32 devices in a mesh: tm: 4 (over z), gx: 2 (over y), gy: 4 (over x, core).
Axes of the slice: x: 2, y: 2, z: 4, core: 2. Of those that a mesh axis runs over, the one named last changes fastest.
Arguments:
- segment_opening_values: float32 [4, 4, 24, 64, 128], P('tm', None, 'gx', 'gy'), may hold values from -6 to 6
- cell_material_label: int32 [24, 64, 128], P('gx', 'gy'), may hold values from 0 to 5
- material_rigidity: float32 [6], replicated, may hold values from 0.3 to 3
- dilation_mismatch: float32 [6], replicated, may hold values from -1 to 1
- heat_swings_array: float32 [4, 2], P('tm'), may hold values from 0.5 to 4
- prony_coefficients: float32 [3], replicated, may hold values from 0.2 to 2
- prony_decay_times: float32 [3], replicated, may hold values from 0.7 to 48
Outputs:
- end_state: float32 [4, 4, 24, 64, 128], P('tm', None, 'gx', 'gy')
The draws below stay inside these ranges and needn't reach their ends.
All inputs are finite; a program needn't handle non-finite values.
Results may differ from the reference program's by a relative error of at most 0.0001.
Values sent between devices are 32-bit elements; how exact they have to be, the bound alone decides.
A program may use at most 64 MiB of HBM per device.

```python
import math
import jax
import jax.numpy as jnp

PRONY = 3
REGIONS = 6
PARTITION_PACES = 2
SHARP_SOLVER_ITER = 3
LOOSE_SOLVER_ITER = 2
STATE = 4
NX = 24
NY = 64
NZ = 128
N_TM = 4


def with_ends(drawn, rng, least, top_value):
    shape = drawn.shape
    place = [jax.random.randint(jax.random.fold_in(rng, axis), (), 0, shape[axis]) for axis in range(len(shape))]
    drawn = drawn.at[tuple(place)].set(least)
    longest = shape.index(max(shape))
    place[longest] = (place[longest] + 1) % shape[longest]
    return drawn.at[tuple(place)].set(top_value)


def level_of(stream_key, extent, pieces, low, high):
    factor_of, own = 1.0, jax.random.fold_in(stream_key, 6)
    for dim, blocks in pieces:
        steps = jnp.exp(jax.random.uniform(jax.random.fold_in(own, dim), (blocks,), jnp.float32, low / len(pieces), high / len(pieces)))
        factor_of = factor_of * jnp.repeat(steps, extent[dim] // blocks).reshape([-1 if axis == dim else 1 for axis in range(len(extent))])
    return factor_of


def normal_values(stream_key, extent, scale, bound, shards=(), held_as=jnp.bfloat16):
    drawn = scale * jax.random.normal(stream_key, extent, jnp.float32)
    if shards:
        drawn = drawn * level_of(stream_key, extent, shards, -0.22, 0.18)
    return jnp.clip(drawn, -bound, bound).astype(held_as)


def setup_inputs(seed: int = 0) -> dict:
    streams_of = jax.random.split(jax.random.key(seed), 8)
    return {
        "segment_opening_values": normal_values(streams_of[0], (N_TM, STATE, NX, NY, NZ), 1.0, 6.0, ((0, 4), (2, 2), (3, 4)), jnp.float32),
        "cell_material_label": with_ends(jax.random.randint(streams_of[1], (NX, NY, NZ), 0, REGIONS), jax.random.fold_in(streams_of[1], 1), 0, REGIONS - 1).astype(jnp.int32),
        "material_rigidity": jnp.clip(jnp.exp(jax.random.uniform(streams_of[2], (REGIONS,), jnp.float32, math.log(0.3), math.log(3.0))), 0.3, 3.0),
        "dilation_mismatch": jnp.clip(jax.random.uniform(streams_of[3], (REGIONS,), jnp.float32, -1.0, 1.0), -1.0, 1.0),
        "heat_swings_array": jnp.clip(0.5 + 3.5 * jax.random.uniform(streams_of[4], (N_TM, PARTITION_PACES), jnp.float32) ** level_of(streams_of[4], (N_TM, PARTITION_PACES), ((0, 4),), -0.2, 0.2), 0.5, 4.0),
        "prony_coefficients": jnp.clip(jnp.exp(jax.random.uniform(streams_of[5], (PRONY,), jnp.float32, math.log(0.2), math.log(2.0))), 0.2, 2.0),
        "prony_decay_times": jnp.clip(jnp.exp(jax.random.uniform(streams_of[6], (PRONY,), jnp.float32, math.log(0.7), math.log(48.0))), 0.7, 48.0),
    }


corners = [(near_one, near_two, near_three) for near_one in (0, 1) for near_two in (0, 1) for near_three in (0, 1)]
diagonal_weights = [1.0 / 3.0] * 8
thermal_weights = [0.25 * (2 * near_three - 1) for near_one, near_two, near_three in corners]


def region_lookup(cell_material_label, region_table):
    looked_up = jnp.zeros(cell_material_label.shape, region_table.dtype)
    for region in range(region_table.shape[0]):
        looked_up = looked_up + jnp.where(cell_material_label == region, region_table[region], jnp.zeros((), region_table.dtype))
    return looked_up


def stencil_apply(padded, cell_rigidity):
    extent_one, extent_two, extent_three = cell_rigidity.shape
    values = [padded[near_one:near_one + extent_one, near_two:near_two + extent_two, near_three:near_three + extent_three] for near_one, near_two, near_three in corners]
    corner_total = values[0]
    for corner_value in values[1:]:
        corner_total = corner_total + corner_value
    result = None
    for corner_index, (near_one, near_two, near_three) in enumerate(corners):
        face_sum = values[corner_index ^ 4] + values[corner_index ^ 2] + values[corner_index ^ 1]
        element_part = cell_rigidity * ((5.0 / 12.0) * values[corner_index] + (face_sum - corner_total) / 12.0)
        node_part = element_part[1 - near_one:extent_one - near_one, 1 - near_two:extent_two - near_two, 1 - near_three:extent_three - near_three]
        result = node_part if result is None else result + node_part
    return result


def nodal_sum(element_field, weights):
    extent_one, extent_two, extent_three = element_field.shape
    result = None
    for corner_index, (near_one, near_two, near_three) in enumerate(corners):
        node_part = weights[corner_index] * element_field[1 - near_one:extent_one - near_one, 1 - near_two:extent_two - near_two, 1 - near_three:extent_three - near_three]
        result = node_part if result is None else result + node_part
    return result


def apply_operator(field, shift_value, cell_rigidity):
    return shift_value * field + stencil_apply(jnp.pad(field, 1), cell_rigidity)


def conjugate_solve(rhs_field, initial, shift_value, diagonal, cell_rigidity, iterations):
    solution = initial
    remainder = rhs_field - apply_operator(solution, shift_value, cell_rigidity)
    scaled = remainder / diagonal
    search = scaled
    gamma_now = jnp.sum(remainder * scaled)
    for iteration in range(iterations):
        image = apply_operator(search, shift_value, cell_rigidity)
        step_size = gamma_now / jnp.sum(search * image)
        solution = solution + step_size * search
        if iteration + 1 < iterations:
            remainder = remainder - step_size * image
            scaled = remainder / diagonal
            gamma_next = jnp.sum(remainder * scaled)
            search = scaled + (gamma_next / gamma_now) * search
            gamma_now = gamma_next
    return solution


def moment_forward(present_displacements, heat_level, step_length, iterations, dilation_deformation, rigidity_main_terms, cell_rigidity, prony_coefficients, prony_decay_times):
    decay_rate = jnp.exp(-step_length / prony_decay_times)
    factors = prony_coefficients * decay_rate
    shift_value = 1.0 / step_length + jnp.sum(factors)
    history = present_displacements[1:]
    rhs_field = present_displacements[0] / step_length + heat_level * dilation_deformation + jnp.sum(factors[:, None, None, None] * history, axis=0)
    displaced = conjugate_solve(rhs_field, present_displacements[0], shift_value, shift_value + rigidity_main_terms, cell_rigidity, iterations)
    history = decay_rate[:, None, None, None] * history + (1.0 - decay_rate)[:, None, None, None] * displaced[None]
    return jnp.concatenate([displaced[None], history], axis=0)


def reference(segment_opening_values, cell_material_label, material_rigidity, dilation_mismatch, heat_swings_array, prony_coefficients, prony_decay_times):
    coefficient = region_lookup(cell_material_label, material_rigidity)
    loaded = coefficient * region_lookup(cell_material_label, dilation_mismatch)
    cell_rigidity = jnp.pad(coefficient, ((1, 0), (1, 0), (1, 0)))
    element_load = jnp.pad(loaded, ((1, 0), (1, 0), (1, 0)))
    dilation_deformation = nodal_sum(element_load, thermal_weights)
    rigidity_main_terms = nodal_sum(cell_rigidity, diagonal_weights)
    loose_interval_span = 1.0 * PARTITION_PACES
    corrections = []
    first_coarse = None
    for segment_number in range(N_TM):
        present_displacements = segment_opening_values[segment_number]
        for sharp_interval_span in range(PARTITION_PACES):
            present_displacements = moment_forward(present_displacements, heat_swings_array[segment_number, sharp_interval_span], 1.0, SHARP_SOLVER_ITER, dilation_deformation, rigidity_main_terms, cell_rigidity, prony_coefficients, prony_decay_times)
        crude_advance_operator = moment_forward(segment_opening_values[segment_number], heat_swings_array[segment_number, PARTITION_PACES - 1], loose_interval_span, LOOSE_SOLVER_ITER, dilation_deformation, rigidity_main_terms, cell_rigidity, prony_coefficients, prony_decay_times)
        corrections.append(present_displacements - crude_advance_operator)
        if segment_number == 0:
            first_coarse = crude_advance_operator
    segment_closing_values = []
    for segment_number in range(N_TM):
        if segment_number == 0:
            crude_prediction = first_coarse
        else:
            crude_prediction = moment_forward(segment_closing_values[-1], heat_swings_array[segment_number, PARTITION_PACES - 1], loose_interval_span, LOOSE_SOLVER_ITER, dilation_deformation, rigidity_main_terms, cell_rigidity, prony_coefficients, prony_decay_times)
        segment_closing_values.append(crude_prediction + corrections[segment_number])
    return jnp.stack(segment_closing_values)
```

```python
import functools

import jax
import jax.numpy as jnp
from jax import lax
from jax.experimental import pallas as pl
from jax.experimental.pallas import tpu as pltpu
from jax.sharding import PartitionSpec as P

PARTITION_PACES = 2
SHARP_SOLVER_ITER = 3
LOOSE_SOLVER_ITER = 2
MESH = pl.DeviceIdType.MESH
F32 = jnp.float32
PAD = 8
UNROLL = 2

LAB, U0, H1, HC, HD, U1, HCP, EU = range(8)
N_HALO = 8
R_FINE1, R_COARSE, R_FINE2, R_CHAIN = range(4)


def kernel(
    sizes,
    state,
    labels,
    rigidity,
    mismatch,
    heat,
    coefs,
    times,
    out,
    lab_x,
    fields,
    kel_b,
    thermal_b,
    sdiag_b,
    inv_fine,
    inv_loose,
    image_b,
    basis,
    part,
    red,
    p_in,
    p_out,
    eu_out,
    u2_b,
    corr_b,
    halo_send,
    halo_recv,
    red_send,
    red_recv,
    tm_send,
    tm_recv,
):
    n_tm, n_gx, n_gy = sizes
    _, prony, nx, ny, nz = state.shape
    prony -= 1
    h = SHARP_SOLVER_ITER + 1
    rows = nx + 2 * h
    wide = ny + 2 * PAD
    tm, gx, gy = lax.axis_index("tm"), lax.axis_index("gx"), lax.axis_index("gy")
    me = gx * n_gy + gy
    own_r = pl.ds(h, nx)
    own_c = pl.ds(PAD, ny)

    def ext(which):
        return lab_x if which == LAB else fields.at[which - 1]

    lab_x[...] = jnp.full(lab_x.shape, -1, jnp.int32)
    zero_row = jnp.zeros((wide, nz), F32)

    def clear(i, carry):
        for which in range(1, N_HALO):
            fields[which - 1, i] = zero_row
        return carry

    lax.fori_loop(0, rows, clear, 0)

    barrier = pltpu.get_barrier_semaphore()
    peers = [(a, b) for a in range(n_gx) for b in range(n_gy)]
    for a, b in peers:

        @pl.when(a * n_gy + b != me)
        def _():
            pl.semaphore_signal(barrier, inc=1, device_id=(tm, a, b), device_id_type=MESH)

    for step in (-1, 1):

        @pl.when((tm + step >= 0) & (tm + step < n_tm))
        def _():
            pl.semaphore_signal(
                barrier, inc=1, device_id=(tm + step, gx, gy), device_id_type=MESH
            )

    def splat(value):
        return jnp.full((1, nz), value, F32)

    def decays(dt):
        decay = [jnp.exp(-dt / splat(times[p])) for p in range(prony)]
        factor = [splat(coefs[p]) * decay[p] for p in range(prony)]
        return decay, factor

    fine_dt, loose_dt = 1.0, 1.0 * PARTITION_PACES
    d_fine, f_fine = decays(fine_dt)
    d_loose, f_loose = decays(loose_dt)
    s_fine = sum(f_fine, splat(1.0 / fine_dt))
    s_loose = sum(f_loose, splat(1.0 / loose_dt))

    def fill(i, carry):
        lab_x[h + i, own_c] = labels[i]
        hist = [state[0, 1 + p, i] for p in range(prony)]
        fields[U0 - 1, h + i, own_c] = state[0, 0, i]
        fields[H1 - 1, h + i, own_c] = sum(f_fine[p] * hist[p] for p in range(prony))
        fields[HC - 1, h + i, own_c] = sum(f_loose[p] * hist[p] for p in range(prony))
        fields[HD - 1, h + i, own_c] = sum(
            f_fine[p] * d_fine[p] * hist[p] for p in range(prony)
        )
        return carry

    lax.fori_loop(0, nx, fill, 0)
    waits = (
        len(peers)
        - 1
        + jnp.where(tm > 0, 1, 0).astype(jnp.int32)
        + jnp.where(tm < n_tm - 1, 1, 0).astype(jnp.int32)
    )
    pl.semaphore_wait(barrier, waits)

    directions = [(a, b) for a in (-1, 0, 1) for b in (-1, 0, 1) if (a, b) != (0, 0)]
    src_r = {-1: pl.ds(h, h), 0: own_r, 1: pl.ds(nx, h)}
    dst_r = {-1: pl.ds(h + nx, h), 0: own_r, 1: pl.ds(0, h)}
    src_c = {-1: pl.ds(PAD, PAD), 0: own_c, 1: pl.ds(ny, PAD)}
    dst_c = {-1: pl.ds(PAD + ny, PAD), 0: own_c, 1: pl.ds(0, PAD)}

    def exists(a, b):
        return (gx + a >= 0) & (gx + a < n_gx) & (gy + b >= 0) & (gy + b < n_gy)

    def halo_copy(which, index):
        a, b = directions[index]
        ref = ext(which)
        return pltpu.make_async_remote_copy(
            src_ref=ref.at[src_r[a], src_c[b]],
            dst_ref=ref.at[dst_r[a], dst_c[b]],
            send_sem=halo_send.at[which, index],
            recv_sem=halo_recv.at[which, index],
            device_id=(tm, gx + a, gy + b),
            device_id_type=MESH,
        )

    def halo_start(*which_all):
        for index, (a, b) in enumerate(directions):

            @pl.when(exists(a, b))
            def _():
                for which in which_all:
                    halo_copy(which, index).start()

    def halo_wait(*which_all):
        for index, (a, b) in enumerate(directions):

            @pl.when(exists(-a, -b))
            def _():
                for which in which_all:
                    halo_copy(which, index).wait_recv()

    def halo_drain(*which_all):
        for index, (a, b) in enumerate(directions):

            @pl.when(exists(a, b))
            def _():
                for which in which_all:
                    halo_copy(which, index).wait_send()

    halo_start(LAB, U0, H1)
    halo_start(HC, HD)

    def red_copy(which, target):
        a, b = peers[target]
        return pltpu.make_async_remote_copy(
            src_ref=part.at[which],
            dst_ref=red.at[which, me],
            send_sem=red_send.at[which, target],
            recv_sem=red_recv.at[which, me],
            device_id=(tm, a, b),
            device_id_type=MESH,
        )

    def red_start(which, sums):
        for j, value in enumerate(sums):
            part[which, j : j + 1] = jnp.sum(value, axis=0, keepdims=True)
        for target in range(len(peers)):

            @pl.when(target != me)
            def _():
                red_copy(which, target).start()

    def red_finish(which, count):
        for source in range(len(peers)):

            @pl.when(source != me)
            def _():
                pltpu.make_async_remote_copy(
                    src_ref=part.at[which],
                    dst_ref=red.at[which, source],
                    send_sem=red_send.at[which, source],
                    recv_sem=red_recv.at[which, source],
                    device_id=(tm, gx, gy),
                    device_id_type=MESH,
                ).wait_recv()

        mine = part[which]
        total = None
        for source in range(len(peers)):
            value = jnp.where(source == me, mine, red[which, source])
            total = value if total is None else total + value
        total = jnp.broadcast_to(jnp.sum(total, axis=1, keepdims=True), total.shape)
        return [total[j : j + 1] for j in range(count)]

    def red_drain(which):
        for target in range(len(peers)):

            @pl.when(target != me)
            def _():
                red_copy(which, target).wait_send()

    lane = lax.broadcasted_iota(jnp.int32, (wide, nz), 1)
    first_lane, last_lane = lane == 0, lane == nz - 1

    def next_z(v):
        return jnp.where(last_lane, 0.0, pltpu.roll(v, nz - 1, 1))

    def prior_z(v):
        return jnp.where(first_lane, 0.0, pltpu.roll(v, 1, 1))

    def next_y(v):
        return pltpu.roll(v, wide - 1, 0)

    def prior_y(v):
        return pltpu.roll(v, 1, 0)

    def forward(v):
        up = next_z(v)
        total, diff = v + up, up - v
        total_up, diff_up = next_y(total), next_y(diff)
        return (total + total_up, diff + diff_up, total_up - total, diff_up - diff)

    def element_row(low, high, k):
        k2 = k + k
        k3 = k2 + k
        g1 = k3 * (high[0] - low[0])
        to_low, to_high = [-g1], [g1]
        for f, weights in ((1, (k3, k2)), (2, (k3, k2)), (3, (k2, k))):
            g0 = weights[0] * (high[f] + low[f])
            g1 = weights[1] * (high[f] - low[f])
            to_low.append(g0 - g1)
            to_high.append(g0 + g1)
        return to_low, to_high

    def backward(g):
        zs = (g[0] - g[2]) + prior_y(g[0] + g[2])
        zd = (g[1] - g[3]) + prior_y(g[1] + g[3])
        return (zs - zd) + prior_z(zs + zd)

    def apply(load, emit, margin, extra):
        low_row, high_row = h - margin, h + nx + margin
        before = forward(load(low_row - 1))
        here = forward(load(low_row))
        _, pending = element_row(before, here, kel_b[low_row - 1])

        def body(e, carry):
            here, pending, extra = carry
            after = forward(load(e + 1))
            to_low, to_high = element_row(here, after, kel_b[e])
            image = backward([x + y for x, y in zip(pending, to_low)])
            extra = emit(e, image, extra)
            return after, tuple(to_high), extra

        _, _, extra = lax.fori_loop(
            low_row, high_row, body, (here, tuple(pending), extra), unroll=UNROLL
        )
        return extra

    zero_sum = jnp.zeros((ny, nz), F32)

    def own(v):
        return v[PAD : PAD + ny]

    def own_weight(e):
        return jnp.where((e >= h) & (e < h + nx), 1.0, 0.0).astype(F32)

    def krylov(iterations, inv_b, level0):
        sums = [level0]
        for k in range(iterations):
            final = k + 1 == iterations

            def emit(e, image, carry):
                v = basis[k, e]
                t = image - sdiag_b[e] * v
                if final:
                    return (carry[0] + own(v * t),)
                v_new = inv_b[e] * t
                basis[k + 1, e] = v_new
                w = own_weight(e)
                t = own(t) * w
                return carry[0] + own(v) * t, carry[1] + own(v_new) * t

            count = 1 if final else 2
            got = apply(
                lambda e: basis[k, e], emit, iterations - 1 - k, (zero_sum,) * count
            )
            sums.extend(got)
        return sums

    def first_level(u_ref, h_ref, u_weight, level, inv_b, margin, keep_image):
        def emit(e, image, carry):
            if keep_image:
                image_b[e] = image
            r = u_weight * u_ref[e] + level * thermal_b[e] + h_ref[e] - image
            v = inv_b[e] * r
            basis[0, e] = v
            return (carry[0] + own(v * r) * own_weight(e),)

        return apply(lambda e: u_ref[e], emit, margin, (zero_sum,))[0]

    def guarded(numerator, denominator):
        good = denominator > 0.0
        return jnp.where(good, numerator / jnp.where(good, denominator, 1.0), 0.0)

    def galerkin(nu, m):
        a = [nu[j] + nu[j + 1] for j in range(2 * m - 1)]
        lower = [[None] * m for _ in range(m)]
        pivots, y = [], []
        for i in range(m):
            row = []
            for j in range(i):
                value = a[i + j]
                for q in range(j):
                    value = value - row[q] * lower[j][q]
                row.append(value)
                lower[i][j] = guarded(value, pivots[j])
            pivot, rhs = a[2 * i], nu[i]
            for q in range(i):
                pivot = pivot - row[q] * lower[i][q]
                rhs = rhs - lower[i][q] * y[q]
            pivots.append(pivot)
            y.append(rhs)
        c = [None] * m
        for i in reversed(range(m)):
            value = guarded(y[i], pivots[i])
            for q in range(i + 1, m):
                value = value - lower[q][i] * c[q]
            c[i] = value
        return c

    def solved(u, c, i):
        for k, weight in enumerate(c):
            u = u + weight * basis[k, h + i, own_c]
        return u

    halo_wait(LAB, U0, H1)
    node_y = gy * ny - PAD + lax.broadcasted_iota(jnp.int32, (wide, nz), 0)
    inside_y = (node_y >= 0) & (node_y < n_gy * ny)

    def coefficients(e):
        ids = lab_x[e]
        kel = jnp.zeros((wide, nz), F32)
        gap = jnp.zeros((wide, nz), F32)
        for region in range(rigidity.shape[0]):
            here = ids == region
            kel = jnp.where(here, rigidity[region], kel)
            gap = jnp.where(here, mismatch[region], gap)
        kal = kel * gap
        return kel, kal

    def nodal(kel, kal):
        kel_y = kel + prior_y(kel)
        kal_y = kal + prior_y(kal)
        return kel_y + prior_z(kel_y), prior_z(kal_y) - kal_y

    kel, kal = coefficients(0)
    kel_b[0] = kel * (1.0 / 48.0)

    def setup(e, carry):
        kel, kal = coefficients(e)
        kel_b[e] = kel * (1.0 / 48.0)
        new = nodal(kel, kal)
        diag = (carry[0] + new[0]) * (1.0 / 3.0)
        sdiag_b[e] = diag
        thermal_b[e] = (carry[1] + new[1]) * 0.25
        node_x = gx * nx - h + e
        inside = jnp.where((node_x >= 0) & (node_x < n_gx * nx), 1.0, 0.0).astype(F32)
        inv_fine[e] = jnp.where(inside_y, inside / (s_fine + diag), 0.0)
        inv_loose[e] = jnp.where(inside_y, inside / (s_loose + diag), 0.0)
        return new

    lax.fori_loop(1, rows, setup, nodal(kel, kal))

    heat_fine = [splat(heat[0, s]) for s in range(PARTITION_PACES)]
    heat_loose = heat_fine[PARTITION_PACES - 1]
    u0_x, u1_x, eu_x = ext(U0), ext(U1), ext(EU)

    level0 = first_level(
        u0_x,
        ext(H1),
        splat(1.0 / fine_dt) - s_fine,
        heat_fine[0],
        inv_fine,
        SHARP_SOLVER_ITER,
        True,
    )
    red_start(R_FINE1, krylov(SHARP_SOLVER_ITER, inv_fine, level0))
    c = galerkin(red_finish(R_FINE1, 2 * SHARP_SOLVER_ITER), SHARP_SOLVER_ITER)

    def end_fine1(i, carry):
        fields[U1 - 1, h + i, own_c] = solved(u0_x[h + i, own_c], c, i)
        return carry

    lax.fori_loop(0, nx, end_fine1, 0)
    halo_start(U1)

    halo_wait(HC, HD)
    h_coarse = ext(HC)

    def coarse_first(e, carry):
        r = (
            (splat(1.0 / loose_dt) - s_loose) * u0_x[e]
            + heat_loose * thermal_b[e]
            + h_coarse[e]
            - image_b[e]
        )
        v = inv_loose[e] * r
        basis[0, e] = v
        return carry + own(v * r) * own_weight(e)

    level0 = lax.fori_loop(
        h - LOOSE_SOLVER_ITER, h + nx + LOOSE_SOLVER_ITER, coarse_first, zero_sum
    )
    red_start(R_COARSE, krylov(LOOSE_SOLVER_ITER, inv_loose, level0))
    c = galerkin(red_finish(R_COARSE, 2 * LOOSE_SOLVER_ITER), LOOSE_SOLVER_ITER)

    keep_fine = [1.0 - d for d in d_fine]
    keep_loose = [1.0 - d for d in d_loose]

    def end_coarse(i, carry):
        u = solved(u0_x[h + i, own_c], c, i)
        corr_b[0, i] = -u
        u1 = u1_x[h + i, own_c]
        for p in range(prony):
            old = state[0, 1 + p, i]
            corr_b[1 + p, i] = -(d_loose[p] * old + keep_loose[p] * u)
            p_out[p, i] = d_fine[p] * (d_fine[p] * old + keep_fine[p] * u1)
        return carry

    lax.fori_loop(0, nx, end_coarse, 0)

    def tm_copy(index, up):
        src = eu_out if index == prony else p_out.at[index]
        dst = eu_x.at[own_r, own_c] if index == prony else p_in.at[index]
        return pltpu.make_async_remote_copy(
            src_ref=src,
            dst_ref=dst,
            send_sem=tm_send.at[index],
            recv_sem=tm_recv.at[index],
            device_id=(tm + up, gx, gy),
            device_id_type=MESH,
        )

    has_next = tm < n_tm - 1

    @pl.when((tm == 0) & has_next)
    def _():
        for p in range(prony):
            tm_copy(p, 1).start()

    halo_wait(U1)
    held = sum((f_fine[p] * d_fine[p] for p in range(prony)), splat(0.0))
    level0 = first_level(
        u1_x, ext(HD), -held, heat_fine[1], inv_fine, SHARP_SOLVER_ITER, False
    )
    red_start(R_FINE2, krylov(SHARP_SOLVER_ITER, inv_fine, level0))
    c_fine = galerkin(red_finish(R_FINE2, 2 * SHARP_SOLVER_ITER), SHARP_SOLVER_ITER)

    @pl.when(tm == 0)
    def _():
        def first_u(i, carry):
            eu_out[i] = solved(u1_x[h + i, own_c], c_fine, i)
            return carry

        lax.fori_loop(0, nx, first_u, 0)

        @pl.when(has_next)
        def _():
            tm_copy(prony, 1).start()

        def first_out(i, carry):
            u2 = eu_out[i]
            out[0, 0, i] = u2
            for p in range(prony):
                out[0, 1 + p, i] = p_out[p, i] + keep_fine[p] * u2
            return carry

        lax.fori_loop(0, nx, first_out, 0)

    @pl.when(tm > 0)
    def _():
        def correct(i, carry):
            u2 = solved(u1_x[h + i, own_c], c_fine, i)
            corr_b[0, i] = corr_b[0, i] + u2
            for p in range(prony):
                corr_b[1 + p, i] = corr_b[1 + p, i] + (p_out[p, i] + keep_fine[p] * u2)
            return carry

        lax.fori_loop(0, nx, correct, 0)

        from_first = tm == 1
        given = [jnp.where(from_first, keep_fine[p], keep_loose[p]) for p in range(prony)]
        for p in range(prony):
            tm_copy(p, -1).wait_recv()

        def combine(i, carry):
            fields[HCP - 1, h + i, own_c] = sum(f_loose[p] * p_in[p, i] for p in range(prony))
            return carry

        lax.fori_loop(0, nx, combine, 0)
        halo_start(HCP)
        tm_copy(prony, -1).wait_recv()
        halo_start(EU)

        def ahead(i, carry):
            u = eu_x[h + i, own_c]
            for p in range(prony):
                old = p_in[p, i] + given[p] * u
                p_out[p, i] = (
                    d_loose[p] * old + corr_b[1 + p, i] - keep_loose[p] * corr_b[0, i]
                )
            return carry

        lax.fori_loop(0, nx, ahead, 0)

        @pl.when(has_next)
        def _():
            for p in range(prony):
                tm_copy(p, 1).start()

        halo_wait(HCP, EU)
        gain = splat(1.0 / loose_dt) - s_loose
        for p in range(prony):
            gain = gain + f_loose[p] * given[p]
        level0 = first_level(
            eu_x, ext(HCP), gain, heat_loose, inv_loose, LOOSE_SOLVER_ITER, False
        )
        red_start(R_CHAIN, krylov(LOOSE_SOLVER_ITER, inv_loose, level0))
        c = galerkin(red_finish(R_CHAIN, 2 * LOOSE_SOLVER_ITER), LOOSE_SOLVER_ITER)

        def last_u(i, carry):
            eu_out[i] = solved(eu_x[h + i, own_c], c, i) + corr_b[0, i]
            return carry

        lax.fori_loop(0, nx, last_u, 0)

        @pl.when(has_next)
        def _():
            tm_copy(prony, 1).start()

        def last_out(i, carry):
            u = eu_out[i]
            out[0, 0, i] = u
            for p in range(prony):
                out[0, 1 + p, i] = p_out[p, i] + keep_loose[p] * u
            return carry

        lax.fori_loop(0, nx, last_out, 0)
        halo_drain(HCP, EU)
        red_drain(R_CHAIN)

    @pl.when(has_next)
    def _():
        for index in range(prony + 1):
            tm_copy(index, 1).wait_send()

    halo_drain(LAB, U0, H1, HC, HD, U1)
    for which in (R_FINE1, R_COARSE, R_FINE2):
        red_drain(which)


def on_device(sizes, state, labels, rigidity, mismatch, heat, coefs, times):
    _, fields, nx, ny, nz = state.shape
    h = SHARP_SOLVER_ITER + 1
    rows, wide = nx + 2 * h, ny + 2 * PAD
    peers = sizes[1] * sizes[2]
    field = (rows, wide, nz)
    own = (nx, ny, nz)
    vmem = pl.BlockSpec(memory_space=pltpu.VMEM)
    smem = pl.BlockSpec(memory_space=pltpu.SMEM)
    dma = pltpu.SemaphoreType.DMA
    return pl.pallas_call(
        functools.partial(kernel, sizes),
        out_shape=jax.ShapeDtypeStruct(state.shape, state.dtype),
        in_specs=[vmem, vmem, smem, smem, smem, smem, smem],
        out_specs=vmem,
        scratch_shapes=[
            pltpu.VMEM(field, jnp.int32),
            pltpu.VMEM((N_HALO - 1,) + field, F32),
            pltpu.VMEM(field, F32),
            pltpu.VMEM(field, F32),
            pltpu.VMEM(field, F32),
            pltpu.VMEM(field, F32),
            pltpu.VMEM(field, F32),
            pltpu.VMEM(field, F32),
            pltpu.VMEM((SHARP_SOLVER_ITER,) + field, F32),
            pltpu.VMEM((4, 8, nz), F32),
            pltpu.VMEM((4, peers, 8, nz), F32),
            pltpu.VMEM((fields - 1,) + own, F32),
            pltpu.VMEM((fields - 1,) + own, F32),
            pltpu.VMEM(own, F32),
            pltpu.VMEM(own, F32),
            pltpu.VMEM((fields,) + own, F32),
            dma((N_HALO, 8)),
            dma((N_HALO, 8)),
            dma((4, peers)),
            dma((4, peers)),
            dma((fields,)),
            dma((fields,)),
        ],
        compiler_params=pltpu.CompilerParams(
            collective_id=0, has_side_effects=True, vmem_limit_bytes=56 * 1024 * 1024
        ),
    )(state, labels, rigidity, mismatch, heat, coefs, times)


def solution(mesh):
    sizes = tuple(mesh.shape[name] for name in ("tm", "gx", "gy"))
    placed = (
        P("tm", None, "gx", "gy", None),
        P("gx", "gy", None),
        P(),
        P(),
        P("tm", None),
        P(),
        P(),
    )
    return jax.shard_map(
        functools.partial(on_device, sizes),
        mesh=mesh,
        in_specs=placed,
        out_specs=P("tm", None, "gx", "gy", None),
        check_vma=False,
    )
```

```python
import functools

import jax
import jax.numpy as jnp
from jax import lax
from jax.experimental import pallas as pl
from jax.experimental.pallas import tpu as pltpu
from jax.sharding import PartitionSpec as P

PARTITION_PACES = 2
SHARP_SOLVER_ITER = 3
LOOSE_SOLVER_ITER = 2
MESH = pl.DeviceIdType.MESH
F32 = jnp.float32
PAD = 8
UNROLL = 4

LAB, U0, H1, HC, HD, U1, HCP, EU = range(8)
N_HALO = 8
FINE_RIM, LOOSE_RIM = SHARP_SOLVER_ITER + 1, LOOSE_SOLVER_ITER + 1
RIM = {
    LAB: FINE_RIM,
    U0: FINE_RIM,
    H1: FINE_RIM - 1,
    HC: LOOSE_RIM - 1,
    HD: FINE_RIM - 1,
    U1: FINE_RIM,
    HCP: LOOSE_RIM - 1,
    EU: LOOSE_RIM,
}
R_FINE1, R_COARSE, R_FINE2, R_CHAIN = range(4)


def chunks_of(nx):
    middle = nx - 2 * LOOSE_RIM
    cut = [(0, LOOSE_RIM), (nx - LOOSE_RIM, LOOSE_RIM)]
    half = middle // 2
    cut += [(LOOSE_RIM, half), (LOOSE_RIM + half, middle - half)]
    return [(start, count) for start, count in cut if count > 0]


def loop(low, high, body, carry):
    return lax.fori_loop(low, high, body, carry, unroll=UNROLL)


def kernel(
    sizes,
    state,
    labels,
    rigidity,
    mismatch,
    heat,
    coefs,
    times,
    out,
    lab_x,
    fields,
    kel_b,
    thermal_b,
    sdiag_b,
    inv_fine,
    inv_loose,
    image_b,
    basis,
    basis_loose,
    part,
    red,
    p_in,
    p_out,
    eu_out,
    u2_b,
    corr_b,
    halo_send,
    halo_recv,
    red_send,
    red_recv,
    tm_send,
    tm_recv,
    side_send,
    side_recv,
):
    n_tm, n_gx, n_gy = sizes
    _, prony, nx, ny, nz = state.shape
    prony -= 1
    h = SHARP_SOLVER_ITER + 1
    rows = nx + 2 * h
    wide = ny + 2 * PAD
    tm, gx, gy = lax.axis_index("tm"), lax.axis_index("gx"), lax.axis_index("gy")
    me = gx * n_gy + gy
    own_r = pl.ds(h, nx)
    own_c = pl.ds(PAD, ny)

    def ext(which):
        return lab_x if which == LAB else fields.at[which - 1]

    lab_x[...] = jnp.full(lab_x.shape, -1, jnp.int32)
    zero_row = jnp.zeros((wide, nz), F32)

    def clear(i, carry):
        for which in range(1, N_HALO):
            fields[which - 1, i] = zero_row
        return carry

    loop(0, rows, clear, 0)
    for row in (h - 1, h + nx):
        for k in range(SHARP_SOLVER_ITER):
            basis[k, row] = zero_row
        for k in range(LOOSE_SOLVER_ITER):
            basis_loose[k, row] = zero_row

    barrier = pltpu.get_barrier_semaphore()
    peers = [(a, b) for a in range(n_gx) for b in range(n_gy)]
    for a, b in peers:

        @pl.when(a * n_gy + b != me)
        def _():
            pl.semaphore_signal(barrier, inc=1, device_id=(tm, a, b), device_id_type=MESH)

    for step in (-1, 1):

        @pl.when((tm + step >= 0) & (tm + step < n_tm))
        def _():
            pl.semaphore_signal(
                barrier, inc=1, device_id=(tm + step, gx, gy), device_id_type=MESH
            )

    def splat(value):
        return jnp.full((1, nz), value, F32)

    def decays(dt):
        decay = [jnp.exp(-dt / splat(times[p])) for p in range(prony)]
        factor = [splat(coefs[p]) * decay[p] for p in range(prony)]
        return decay, factor

    fine_dt, loose_dt = 1.0, 1.0 * PARTITION_PACES
    d_fine, f_fine = decays(fine_dt)
    d_loose, f_loose = decays(loose_dt)
    s_fine = sum(f_fine, splat(1.0 / fine_dt))
    s_loose = sum(f_loose, splat(1.0 / loose_dt))

    def fill(i, carry):
        lab_x[h + i, own_c] = labels[i]
        hist = [state[0, 1 + p, i] for p in range(prony)]
        fields[U0 - 1, h + i, own_c] = state[0, 0, i]
        fields[H1 - 1, h + i, own_c] = sum(f_fine[p] * hist[p] for p in range(prony))
        fields[HC - 1, h + i, own_c] = sum(f_loose[p] * hist[p] for p in range(prony))
        fields[HD - 1, h + i, own_c] = sum(
            f_fine[p] * d_fine[p] * hist[p] for p in range(prony)
        )
        return carry

    loop(0, nx, fill, 0)
    waits = (
        len(peers)
        - 1
        + jnp.where(tm > 0, 1, 0).astype(jnp.int32)
        + jnp.where(tm < n_tm - 1, 1, 0).astype(jnp.int32)
    )
    pl.semaphore_wait(barrier, waits)

    directions = [(a, b) for a in (-1, 0, 1) for b in (-1, 0, 1) if (a, b) != (0, 0)]

    def src_r(a, w):
        return {-1: pl.ds(h, w), 0: own_r, 1: pl.ds(h + nx - w, w)}[a]

    def dst_r(a, w):
        return {-1: pl.ds(h + nx, w), 0: own_r, 1: pl.ds(h - w, w)}[a]

    src_c = {-1: pl.ds(PAD, PAD), 0: own_c, 1: pl.ds(ny, PAD)}
    dst_c = {-1: pl.ds(PAD + ny, PAD), 0: own_c, 1: pl.ds(0, PAD)}

    def exists(a, b):
        return (gx + a >= 0) & (gx + a < n_gx) & (gy + b >= 0) & (gy + b < n_gy)

    def halo_copy(which, index):
        a, b = directions[index]
        ref = ext(which)
        return pltpu.make_async_remote_copy(
            src_ref=ref.at[src_r(a, RIM[which]), src_c[b]],
            dst_ref=ref.at[dst_r(a, RIM[which]), dst_c[b]],
            send_sem=halo_send.at[which, index],
            recv_sem=halo_recv.at[which, index],
            device_id=(tm, gx + a, gy + b),
            device_id_type=MESH,
        )

    def halo_start(*which_all):
        for index, (a, b) in enumerate(directions):

            @pl.when(exists(a, b))
            def _():
                for which in which_all:
                    halo_copy(which, index).start()

    def halo_wait(*which_all):
        for index, (a, b) in enumerate(directions):

            @pl.when(exists(-a, -b))
            def _():
                for which in which_all:
                    halo_copy(which, index).wait_recv()

    def halo_drain(*which_all):
        for index, (a, b) in enumerate(directions):

            @pl.when(exists(a, b))
            def _():
                for which in which_all:
                    halo_copy(which, index).wait_send()

    halo_start(LAB, U0, H1)
    halo_start(HC, HD)

    def red_copy(which, target):
        a, b = peers[target]
        return pltpu.make_async_remote_copy(
            src_ref=part.at[which],
            dst_ref=red.at[which, me],
            send_sem=red_send.at[which, target],
            recv_sem=red_recv.at[which, me],
            device_id=(tm, a, b),
            device_id_type=MESH,
        )

    def red_start(which, sums):
        for j, value in enumerate(sums):
            part[which, j : j + 1] = jnp.sum(value, axis=0, keepdims=True)
        for target in range(len(peers)):

            @pl.when(target != me)
            def _():
                red_copy(which, target).start()

    def red_finish(which, count):
        for source in range(len(peers)):

            @pl.when(source != me)
            def _():
                pltpu.make_async_remote_copy(
                    src_ref=part.at[which],
                    dst_ref=red.at[which, source],
                    send_sem=red_send.at[which, source],
                    recv_sem=red_recv.at[which, source],
                    device_id=(tm, gx, gy),
                    device_id_type=MESH,
                ).wait_recv()

        mine = part[which]
        total = None
        for source in range(len(peers)):
            value = jnp.where(source == me, mine, red[which, source])
            total = value if total is None else total + value
        total = jnp.broadcast_to(jnp.sum(total, axis=1, keepdims=True), total.shape)
        return [total[j : j + 1] for j in range(count)]

    def red_drain(which):
        for target in range(len(peers)):

            @pl.when(target != me)
            def _():
                red_copy(which, target).wait_send()

    lane = lax.broadcasted_iota(jnp.int32, (wide, nz), 1)
    first_lane, last_lane = lane == 0, lane == nz - 1

    def next_z(v):
        return jnp.where(last_lane, 0.0, pltpu.roll(v, nz - 1, 1))

    def prior_z(v):
        return jnp.where(first_lane, 0.0, pltpu.roll(v, 1, 1))

    def next_y(v):
        return pltpu.roll(v, wide - 1, 0)

    def prior_y(v):
        return pltpu.roll(v, 1, 0)

    def forward(v):
        up = next_z(v)
        total, diff = v + up, up - v
        total_up, diff_up = next_y(total), next_y(diff)
        return (total + total_up, diff + diff_up, total_up - total, diff_up - diff)

    def element_row(low, high, k):
        k2 = k + k
        k3 = k2 + k
        g1 = k3 * (high[0] - low[0])
        to_low, to_high = [-g1], [g1]
        for f, weights in ((1, (k3, k2)), (2, (k3, k2)), (3, (k2, k))):
            g0 = weights[0] * (high[f] + low[f])
            g1 = weights[1] * (high[f] - low[f])
            to_low.append(g0 - g1)
            to_high.append(g0 + g1)
        return to_low, to_high

    def backward(g):
        zs = (g[0] - g[2]) + prior_y(g[0] + g[2])
        zd = (g[1] - g[3]) + prior_y(g[1] + g[3])
        return (zs - zd) + prior_z(zs + zd)

    def span(margin):
        if n_gx == 1:
            return h, nx
        if n_gx == 2:
            return h - margin * gx, nx + margin
        return h - margin, nx + 2 * margin

    def apply(load, emit, margin, extra):
        low_row, count = span(margin)
        before = forward(load(low_row - 1))
        here = forward(load(low_row))
        _, pending = element_row(before, here, kel_b[low_row - 1])

        def body(t, carry):
            here, pending, extra = carry
            e = low_row + t
            after = forward(load(e + 1))
            to_low, to_high = element_row(here, after, kel_b[e])
            image = backward([x + y for x, y in zip(pending, to_low)])
            extra = emit(e, image, extra)
            return after, tuple(to_high), extra

        _, _, extra = lax.fori_loop(
            0, count, body, (here, tuple(pending), extra), unroll=True
        )
        return extra

    zero_sum = jnp.zeros((ny, nz), F32)

    def own(v):
        return v[PAD : PAD + ny]

    def own_weight(e):
        return jnp.where((e >= h) & (e < h + nx), 1.0, 0.0).astype(F32)

    def krylov(iterations, basis, inv_b, level0):
        sums = [level0]
        for k in range(iterations):
            final = k + 1 == iterations

            def emit(e, image, carry):
                v = basis[k, e]
                t = image - sdiag_b[e] * v
                if final:
                    return (carry[0] + own(v * t),)
                v_new = inv_b[e] * t
                basis[k + 1, e] = v_new
                w = own_weight(e)
                t = own(t) * w
                return carry[0] + own(v) * t, carry[1] + own(v_new) * t

            count = 1 if final else 2
            got = apply(
                lambda e: basis[k, e], emit, iterations - 1 - k, (zero_sum,) * count
            )
            sums.extend(got)
        return sums

    def first_level(u_ref, h_ref, u_weight, level, inv_b, margin, keep_image):
        def emit(e, image, carry):
            if keep_image:
                image_b[e] = image
            r = u_weight * u_ref[e] + level * thermal_b[e] + h_ref[e] - image
            v = inv_b[e] * r
            basis[0, e] = v
            return (carry[0] + own(v * r) * own_weight(e),)

        return apply(lambda e: u_ref[e], emit, margin, (zero_sum,))[0]

    def guarded(numerator, denominator):
        good = denominator > 0.0
        return jnp.where(good, numerator / jnp.where(good, denominator, 1.0), 0.0)

    def galerkin(nu, m):
        a = [nu[j] + nu[j + 1] for j in range(2 * m - 1)]
        lower = [[None] * m for _ in range(m)]
        pivots, y = [], []
        for i in range(m):
            row = []
            for j in range(i):
                value = a[i + j]
                for q in range(j):
                    value = value - row[q] * lower[j][q]
                row.append(value)
                lower[i][j] = guarded(value, pivots[j])
            pivot, rhs = a[2 * i], nu[i]
            for q in range(i):
                pivot = pivot - row[q] * lower[i][q]
                rhs = rhs - lower[i][q] * y[q]
            pivots.append(pivot)
            y.append(rhs)
        c = [None] * m
        for i in reversed(range(m)):
            value = guarded(y[i], pivots[i])
            for q in range(i + 1, m):
                value = value - lower[q][i] * c[q]
            c[i] = value
        return c

    def solved(u, c, i, basis=basis):
        for k, weight in enumerate(c):
            u = u + weight * basis[k, h + i, own_c]
        return u

    halo_wait(LAB, U0, H1)
    node_y = gy * ny - PAD + lax.broadcasted_iota(jnp.int32, (wide, nz), 0)
    inside_y = (node_y >= 0) & (node_y < n_gy * ny)

    def coefficients(e):
        ids = lab_x[e]
        kel = jnp.zeros((wide, nz), F32)
        gap = jnp.zeros((wide, nz), F32)
        for region in range(rigidity.shape[0]):
            here = ids == region
            kel = jnp.where(here, rigidity[region], kel)
            gap = jnp.where(here, mismatch[region], gap)
        kal = kel * gap
        return kel, kal

    def nodal(kel, kal):
        kel_y = kel + prior_y(kel)
        kal_y = kal + prior_y(kal)
        return kel_y + prior_z(kel_y), prior_z(kal_y) - kal_y

    kel, kal = coefficients(0)
    kel_b[0] = kel * (1.0 / 48.0)

    def setup(e, carry):
        kel, kal = coefficients(e)
        kel_b[e] = kel * (1.0 / 48.0)
        new = nodal(kel, kal)
        diag = (carry[0] + new[0]) * (1.0 / 3.0)
        sdiag_b[e] = diag
        thermal_b[e] = (carry[1] + new[1]) * 0.25
        node_x = gx * nx - h + e
        inside = jnp.where((node_x >= 0) & (node_x < n_gx * nx), 1.0, 0.0).astype(F32)
        inv_fine[e] = jnp.where(inside_y, inside / (s_fine + diag), 0.0)
        inv_loose[e] = jnp.where(inside_y, inside / (s_loose + diag), 0.0)
        return new

    loop(1, rows, setup, nodal(kel, kal))

    heat_fine = [splat(heat[0, s]) for s in range(PARTITION_PACES)]
    heat_loose = heat_fine[PARTITION_PACES - 1]
    u0_x, u1_x, eu_x = ext(U0), ext(U1), ext(EU)

    level0 = first_level(
        u0_x,
        ext(H1),
        splat(1.0 / fine_dt) - s_fine,
        heat_fine[0],
        inv_fine,
        SHARP_SOLVER_ITER,
        True,
    )
    red_start(R_FINE1, krylov(SHARP_SOLVER_ITER, basis, inv_fine, level0))

    halo_wait(HC)
    h_coarse = ext(HC)
    coarse_low, coarse_count = span(LOOSE_SOLVER_ITER)

    def coarse_first(t, carry):
        e = coarse_low + t
        r = (
            (splat(1.0 / loose_dt) - s_loose) * u0_x[e]
            + heat_loose * thermal_b[e]
            + h_coarse[e]
            - image_b[e]
        )
        v = inv_loose[e] * r
        basis_loose[0, e] = v
        return carry + own(v * r) * own_weight(e)

    level0 = loop(0, coarse_count, coarse_first, zero_sum)
    red_start(R_COARSE, krylov(LOOSE_SOLVER_ITER, basis_loose, inv_loose, level0))

    c = galerkin(red_finish(R_FINE1, 2 * SHARP_SOLVER_ITER), SHARP_SOLVER_ITER)

    def end_fine1(i, carry):
        fields[U1 - 1, h + i, own_c] = solved(u0_x[h + i, own_c], c, i)
        return carry

    loop(0, nx, end_fine1, 0)
    halo_start(U1)

    keep_fine = [1.0 - d for d in d_fine]
    keep_loose = [1.0 - d for d in d_loose]

    def give_fine(i, carry):
        u1 = u1_x[h + i, own_c]
        for p in range(prony):
            p_out[p, i] = d_fine[p] * (
                d_fine[p] * state[0, 1 + p, i] + keep_fine[p] * u1
            )
        return carry

    loop(0, nx, give_fine, 0)

    chunks = chunks_of(nx)

    def tm_copy(index, up):
        if index < prony:
            src, dst = p_out.at[index], p_in.at[index]
        else:
            start, count = chunks[index - prony]
            src = eu_out.at[pl.ds(start, count)]
            dst = eu_x.at[pl.ds(h + start, count), own_c]
        return pltpu.make_async_remote_copy(
            src_ref=src,
            dst_ref=dst,
            send_sem=tm_send.at[index],
            recv_sem=tm_recv.at[index],
            device_id=(tm + up, gx, gy),
            device_id_type=MESH,
        )

    def side_copy(index, side):
        start, count = chunks[index]
        b = (-1, 1)[side]
        at = pl.ds(h + start, count)
        return pltpu.make_async_remote_copy(
            src_ref=eu_x.at[at, src_c[b]],
            dst_ref=eu_x.at[at, dst_c[b]],
            send_sem=side_send.at[index, side],
            recv_sem=side_recv.at[index, side],
            device_id=(tm, gx, gy + b),
            device_id_type=MESH,
        )

    def end_wait():
        for side, b in enumerate((-1, 1)):

            @pl.when(exists(0, -b))
            def _():
                for index in range(len(chunks)):
                    side_copy(index, side).wait_recv()

        for corner, (a, b) in enumerate(directions):
            if a != 0:

                @pl.when(exists(-a, -b))
                def _():
                    halo_copy(EU, corner).wait_recv()

    def end_drain():
        for side, b in enumerate((-1, 1)):

            @pl.when(exists(0, b))
            def _():
                for index in range(len(chunks)):
                    side_copy(index, side).wait_send()

        for corner, (a, b) in enumerate(directions):
            if a != 0:

                @pl.when(exists(a, b))
                def _():
                    halo_copy(EU, corner).wait_send()

    has_next = tm < n_tm - 1

    @pl.when((tm == 0) & has_next)
    def _():
        for p in range(prony):
            tm_copy(p, 1).start()

    c = galerkin(red_finish(R_COARSE, 2 * LOOSE_SOLVER_ITER), LOOSE_SOLVER_ITER)

    def end_coarse(i, carry):
        u = solved(u0_x[h + i, own_c], c, i, basis_loose)
        corr_b[0, i] = -u
        for p in range(prony):
            corr_b[1 + p, i] = -(d_loose[p] * state[0, 1 + p, i] + keep_loose[p] * u)
        return carry

    loop(0, nx, end_coarse, 0)

    halo_wait(HD, U1)
    held = sum((f_fine[p] * d_fine[p] for p in range(prony)), splat(0.0))
    level0 = first_level(
        u1_x, ext(HD), -held, heat_fine[1], inv_fine, SHARP_SOLVER_ITER, False
    )
    red_start(R_FINE2, krylov(SHARP_SOLVER_ITER, basis, inv_fine, level0))
    c_fine = galerkin(red_finish(R_FINE2, 2 * SHARP_SOLVER_ITER), SHARP_SOLVER_ITER)

    @pl.when(tm == 0)
    def _():
        def first_u(i, carry):
            eu_out[i] = solved(u1_x[h + i, own_c], c_fine, i)
            return carry

        for index, (start, count) in enumerate(chunks):
            loop(start, start + count, first_u, 0)

            @pl.when(has_next)
            def _():
                tm_copy(prony + index, 1).start()

        def first_out(i, carry):
            u2 = eu_out[i]
            out[0, 0, i] = u2
            for p in range(prony):
                out[0, 1 + p, i] = p_out[p, i] + keep_fine[p] * u2
            return carry

        loop(0, nx, first_out, 0)

    @pl.when(tm > 0)
    def _():
        def correct(i, carry):
            u2 = solved(u1_x[h + i, own_c], c_fine, i)
            corr_b[0, i] = corr_b[0, i] + u2
            for p in range(prony):
                corr_b[1 + p, i] = corr_b[1 + p, i] + (p_out[p, i] + keep_fine[p] * u2)
            return carry

        loop(0, nx, correct, 0)

        from_first = tm == 1
        given = [jnp.where(from_first, keep_fine[p], keep_loose[p]) for p in range(prony)]
        for p in range(prony):
            tm_copy(p, -1).wait_recv()

        def combine(i, carry):
            fields[HCP - 1, h + i, own_c] = sum(f_loose[p] * p_in[p, i] for p in range(prony))
            return carry

        loop(0, nx, combine, 0)
        halo_start(HCP)
        for index in range(len(chunks)):
            tm_copy(prony + index, -1).wait_recv()
            for side, b in enumerate((-1, 1)):

                @pl.when(exists(0, b))
                def _():
                    side_copy(index, side).start()

            if index < 2:
                for corner, (a, b) in enumerate(directions):
                    if a == (-1, 1)[index]:

                        @pl.when(exists(a, b))
                        def _():
                            halo_copy(EU, corner).start()

        def ahead(i, carry):
            u = eu_x[h + i, own_c]
            for p in range(prony):
                old = p_in[p, i] + given[p] * u
                p_out[p, i] = (
                    d_loose[p] * old + corr_b[1 + p, i] - keep_loose[p] * corr_b[0, i]
                )
            return carry

        loop(0, nx, ahead, 0)

        @pl.when(has_next)
        def _():
            for p in range(prony):
                tm_copy(p, 1).start()

        halo_wait(HCP)
        end_wait()
        gain = splat(1.0 / loose_dt) - s_loose
        for p in range(prony):
            gain = gain + f_loose[p] * given[p]
        level0 = first_level(
            eu_x, ext(HCP), gain, heat_loose, inv_loose, LOOSE_SOLVER_ITER, False
        )
        red_start(R_CHAIN, krylov(LOOSE_SOLVER_ITER, basis, inv_loose, level0))
        c = galerkin(red_finish(R_CHAIN, 2 * LOOSE_SOLVER_ITER), LOOSE_SOLVER_ITER)

        def last_u(i, carry):
            eu_out[i] = solved(eu_x[h + i, own_c], c, i) + corr_b[0, i]
            return carry

        for index, (start, count) in enumerate(chunks):
            loop(start, start + count, last_u, 0)

            @pl.when(has_next)
            def _():
                tm_copy(prony + index, 1).start()

        def last_out(i, carry):
            u = eu_out[i]
            out[0, 0, i] = u
            for p in range(prony):
                out[0, 1 + p, i] = p_out[p, i] + keep_loose[p] * u
            return carry

        loop(0, nx, last_out, 0)
        halo_drain(HCP)
        end_drain()
        red_drain(R_CHAIN)

    @pl.when(has_next)
    def _():
        for index in range(prony + len(chunks)):
            tm_copy(index, 1).wait_send()

    halo_drain(LAB, U0, H1, HC, HD, U1)
    for which in (R_FINE1, R_COARSE, R_FINE2):
        red_drain(which)


def on_device(sizes, state, labels, rigidity, mismatch, heat, coefs, times):
    _, fields, nx, ny, nz = state.shape
    h = SHARP_SOLVER_ITER + 1
    rows, wide = nx + 2 * h, ny + 2 * PAD
    peers = sizes[1] * sizes[2]
    steps = len(chunks_of(nx))
    field = (rows, wide, nz)
    own = (nx, ny, nz)
    vmem = pl.BlockSpec(memory_space=pltpu.VMEM)
    smem = pl.BlockSpec(memory_space=pltpu.SMEM)
    dma = pltpu.SemaphoreType.DMA
    return pl.pallas_call(
        functools.partial(kernel, sizes),
        out_shape=jax.ShapeDtypeStruct(state.shape, state.dtype),
        in_specs=[vmem, vmem, smem, smem, smem, smem, smem],
        out_specs=vmem,
        scratch_shapes=[
            pltpu.VMEM(field, jnp.int32),
            pltpu.VMEM((N_HALO - 1,) + field, F32),
            pltpu.VMEM(field, F32),
            pltpu.VMEM(field, F32),
            pltpu.VMEM(field, F32),
            pltpu.VMEM(field, F32),
            pltpu.VMEM(field, F32),
            pltpu.VMEM(field, F32),
            pltpu.VMEM((SHARP_SOLVER_ITER,) + field, F32),
            pltpu.VMEM((LOOSE_SOLVER_ITER,) + field, F32),
            pltpu.VMEM((4, 8, nz), F32),
            pltpu.VMEM((4, peers, 8, nz), F32),
            pltpu.VMEM((fields - 1,) + own, F32),
            pltpu.VMEM((fields - 1,) + own, F32),
            pltpu.VMEM(own, F32),
            pltpu.VMEM(own, F32),
            pltpu.VMEM((fields,) + own, F32),
            dma((N_HALO, 8)),
            dma((N_HALO, 8)),
            dma((4, peers)),
            dma((4, peers)),
            dma((fields - 1 + steps,)),
            dma((fields - 1 + steps,)),
            dma((steps, 2)),
            dma((steps, 2)),
        ],
        compiler_params=pltpu.CompilerParams(
            collective_id=0, has_side_effects=True, vmem_limit_bytes=56 * 1024 * 1024
        ),
    )(state, labels, rigidity, mismatch, heat, coefs, times)


def solution(mesh):
    sizes = tuple(mesh.shape[name] for name in ("tm", "gx", "gy"))
    placed = (
        P("tm", None, "gx", "gy", None),
        P("gx", "gy", None),
        P(),
        P(),
        P("tm", None),
        P(),
        P(),
    )
    return jax.shard_map(
        functools.partial(on_device, sizes),
        mesh=mesh,
        in_specs=placed,
        out_specs=P("tm", None, "gx", "gy", None),
        check_vma=False,
    )
```
